128 devices in a mesh: seq: 32 (over y, x, core), tp: 4 (over z).
Axes of the slice: x: 4, y: 4, z: 4, core: 2. Of those that a mesh axis runs over, the one named last changes fastest.
Arguments:
- short_inputs: bfloat16 [4, 10240, 1280], P(None, 'seq'), may hold values from -8 to 8
- long_inputs: bfloat16 [4, 12, 1280], replicated, may hold values from -8 to 8
- short_keys: bfloat16 [10240, 16, 1280], P('seq', None, 'tp'), may hold values from -6 to 6
- short_values: bfloat16 [10240, 16, 1280], P('seq', None, 'tp'), may hold values from -6 to 6
- long_keys: bfloat16 [12, 512, 1280], P(None, 'seq', 'tp'), may hold values from -6 to 6
- long_values: bfloat16 [12, 512, 1280], P(None, 'seq', 'tp'), may hold values from -6 to 6
- short_lengths: int32 [10240], P('seq'), may hold values from 1 to 16, as said below
- long_lengths: int32 [12], replicated, may hold values from 128 to 512, as said below
- attn_gain: float32 [1280], replicated, may hold values from 0.1 to 1.9
- mlp_gain: float32 [1280], replicated, may hold values from 0.1 to 1.9
- query_scale: float32 [16, 80], P('tp'), may hold values from 1 to 40, as said below
- q_weight: bfloat16 [1280, 1280], P(None, 'tp'), may hold values from -0.15625 to 0.15625
- k_weight: bfloat16 [1280, 1280], P(None, 'tp'), may hold values from -0.15625 to 0.15625
- v_weight: bfloat16 [1280, 1280], P(None, 'tp'), may hold values from -0.15625 to 0.15625
- o_weight: bfloat16 [1280, 1280], P('tp'), may hold values from -0.15625 to 0.15625
- up_weight: bfloat16 [1280, 1280], P(None, 'tp'), may hold values from -0.15625 to 0.15625
- down_weight: bfloat16 [1280, 1280], P('tp'), may hold values from -0.15625 to 0.15625
Outputs:
- short_outputs: bfloat16 [4, 10240, 1280], P(None, 'seq', 'tp')
- long_outputs: bfloat16 [4, 12, 1280], P(None, None, 'tp')
The draws below stay inside these ranges and needn't reach their ends.
Inputs may be any that keep to these rules, and one draw needn't show every extreme that they name: `short_lengths`: some short request fills all 16 slots. `long_lengths`: some long request fills all 512 slots. `query_scale`: positive scales.
All inputs are finite; a program needn't handle non-finite values.
Results may differ from the reference program's by a relative error of at most 0.012.
The reference program's roundings to bfloat16 on the way count: a program that leaves them out, or rounds other values in their place, can miss the bound.
Values may be sent and summed in bfloat16 or wider, within the bound.
A program may use at most 128 MiB of HBM per device.

```python
import math
import jax
import jax.numpy as jnp
from jax import lax

D = 1280
H = 16
HD = 80
FF = 1280
STEPS = 4
SHORT_CAP = 16
B_LONG = 12
B_SHORT = 10240
LONG_CAP = 512


def feature_rows(key, row_shape):
    base_key, jitter_key = jax.random.split(key)
    position = jnp.arange(D, dtype=jnp.float32) / (D - 1)
    jitter = jnp.exp(jax.random.uniform(jitter_key, (D,), jnp.float32, math.log(0.8), math.log(1.25)))
    ramp = 0.5 * jnp.exp(math.log(3.0) * position)
    noise = jax.random.normal(base_key, row_shape + (D,), jnp.float32)
    return jnp.clip(noise * ramp * jitter, -8.0, 8.0)


def draw_short_inputs(key, part):
    return feature_rows(jax.random.fold_in(key, 41), (STEPS, B_SHORT)).astype(jnp.bfloat16)


def draw_long_inputs(key, part):
    return feature_rows(jax.random.fold_in(key, 43), (STEPS, B_LONG)).astype(jnp.bfloat16)


def draw_short_lengths(key, part):
    first_key, second_key = jax.random.split(jax.random.fold_in(key, 11))
    values = jax.random.randint(first_key, (B_SHORT,), 1, SHORT_CAP + 1)
    spot_index = jax.random.randint(second_key, (), 0, B_SHORT)
    return values.at[spot_index].set(SHORT_CAP).astype(jnp.int32)


def draw_long_lengths(key, part):
    first_key, second_key = jax.random.split(jax.random.fold_in(key, 23))
    values = jax.random.randint(first_key, (B_LONG,), LONG_CAP // 4, LONG_CAP + 1)
    spot_index = jax.random.randint(second_key, (), 0, B_LONG)
    return values.at[spot_index].set(LONG_CAP).astype(jnp.int32)


def draw_query_scale(key, part):
    uniform_draw = jax.random.uniform(jax.random.fold_in(key, 37), (H, HD), jnp.float32)
    high_log = math.log(6.0)
    return jnp.exp(high_log * uniform_draw).astype(jnp.float32)


def levels(stream_key, shape, cuts, smallest, largest):
    gain, own = 1.0, jax.random.fold_in(stream_key, 6)
    for axis_at, parts in cuts:
        draws = jnp.exp(jax.random.uniform(jax.random.fold_in(own, axis_at), (parts,), jnp.float32, smallest / len(cuts), largest / len(cuts)))
        gain = gain * jnp.repeat(draws, shape[axis_at] // parts).reshape([-1 if axis == axis_at else 1 for axis in range(len(shape))])
    return gain


def gaussian(own_key, extent, scale, most, cuts=(), kind=jnp.bfloat16):
    values = scale * jax.random.normal(own_key, extent, jnp.float32)
    if cuts:
        values = values * levels(own_key, extent, cuts, -0.22, 0.18)
    return jnp.clip(values, -most, most).astype(kind)


def setup_inputs(seed: int = 0) -> dict:
    seeds = jax.random.split(jax.random.key(seed), 18)
    short_inputs = draw_short_inputs(jax.random.fold_in(seeds[17], 71), 0)
    long_inputs = draw_long_inputs(jax.random.fold_in(seeds[17], 71), 0)
    short_keys = gaussian(seeds[2], (B_SHORT, SHORT_CAP, H * HD), 1.0, 6.0, ((0, 32), (2, 4)))
    short_values = gaussian(seeds[3], (B_SHORT, SHORT_CAP, H * HD), 1.0, 6.0, ((0, 32), (2, 4)))
    long_keys = gaussian(seeds[4], (B_LONG, LONG_CAP, H * HD), 1.0, 6.0, ((1, 32), (2, 4)))
    long_values = gaussian(seeds[5], (B_LONG, LONG_CAP, H * HD), 1.0, 6.0, ((1, 32), (2, 4)))
    short_lengths = draw_short_lengths(jax.random.fold_in(seeds[17], 71), 0)
    long_lengths = draw_long_lengths(jax.random.fold_in(seeds[17], 71), 0)
    attn_gain = jnp.clip(1.0 + 0.18 * jax.random.normal(seeds[8], (D,), jnp.float32), 0.1, 1.9)
    mlp_gain = jnp.clip(1.0 + 0.18 * jax.random.normal(seeds[9], (D,), jnp.float32), 0.1, 1.9)
    query_scale = draw_query_scale(jax.random.fold_in(seeds[17], 71), 0)
    q_weight = gaussian(seeds[11], (D, H * HD), D ** -0.5, 0.15625, ((1, 4),))
    k_weight = gaussian(seeds[12], (D, H * HD), D ** -0.5, 0.15625, ((1, 4),))
    v_weight = gaussian(seeds[13], (D, H * HD), D ** -0.5, 0.15625, ((1, 4),))
    o_weight = gaussian(seeds[14], (H * HD, D), (H * HD) ** -0.5, 0.15625, ((0, 4),))
    up_weight = gaussian(seeds[15], (D, FF), D ** -0.5, 0.15625, ((1, 4),))
    down_weight = gaussian(seeds[16], (FF, D), FF ** -0.5, 0.15625, ((0, 4),))
    return dict(short_inputs=short_inputs, long_inputs=long_inputs, short_keys=short_keys, short_values=short_values, long_keys=long_keys, long_values=long_values, short_lengths=short_lengths, long_lengths=long_lengths, attn_gain=attn_gain, mlp_gain=mlp_gain, query_scale=query_scale, q_weight=q_weight, k_weight=k_weight, v_weight=v_weight, o_weight=o_weight, up_weight=up_weight, down_weight=down_weight)


norm_eps = 1e-06
masked_fill = -1e+30

def rms_scale(matrix, gain_row):
    mean_square = lax.optimization_barrier(jnp.sum(matrix * matrix, axis=-1, keepdims=True)) / matrix.shape[-1]
    return matrix * lax.rsqrt(mean_square + norm_eps) * gain_row

def project_heads(flat_rows, weight, step_count, head_count):
    product = jnp.dot(flat_rows, weight, preferred_element_type=jnp.float32)
    return product.reshape(step_count, -1, head_count, product.shape[-1] // head_count)

def attend_group(queries, cache_keys, cache_values, lengths, new_keys, new_values):
    step_count = queries.shape[0]
    head_count, head_dim = (queries.shape[2], queries.shape[3])
    causal = jnp.arange(step_count)[None, :] <= jnp.arange(step_count)[:, None]

    def attend_one(request):
        own_queries, own_keys, own_values, length, own_new_keys, own_new_values = request
        keys_wide = own_keys.astype(jnp.float32).reshape(own_keys.shape[0], head_count, head_dim)
        values_wide = own_values.astype(jnp.float32).reshape(own_values.shape[0], head_count, head_dim)
        queries_wide = own_queries.astype(jnp.float32)
        cache_scores = jnp.einsum('shd,chd->shc', queries_wide, keys_wide)
        valid_slots = jnp.arange(own_keys.shape[0]) < length
        cache_scores = jnp.where(valid_slots, cache_scores, masked_fill)
        fresh_scores = jnp.einsum('shd,thd->sht', queries_wide, own_new_keys.astype(jnp.float32))
        fresh_mask = causal[:, None, :]
        fresh_scores = jnp.where(fresh_mask, fresh_scores, masked_fill)
        row_max = jnp.maximum(lax.optimization_barrier(jnp.max(cache_scores, axis=-1)), lax.optimization_barrier(jnp.max(fresh_scores, axis=-1)))
        cache_probs = jnp.where(valid_slots, jnp.exp(cache_scores - row_max[..., None]), 0.0)
        fresh_probs = jnp.where(fresh_mask, jnp.exp(fresh_scores - row_max[..., None]), 0.0)
        denominator = lax.optimization_barrier(jnp.sum(cache_probs, axis=-1)) + lax.optimization_barrier(jnp.sum(fresh_probs, axis=-1))
        cache_low = lax.optimization_barrier(cache_probs.astype(jnp.bfloat16)).astype(jnp.float32)
        fresh_low = lax.optimization_barrier(fresh_probs.astype(jnp.bfloat16)).astype(jnp.float32)
        weighted = jnp.einsum('shc,chd->shd', cache_low, values_wide)
        weighted = weighted + jnp.einsum('sht,thd->shd', fresh_low, own_new_values.astype(jnp.float32))
        return (weighted / denominator[..., None]).astype(jnp.bfloat16)
    stacked = lax.map(attend_one, (jnp.swapaxes(queries, 0, 1), cache_keys, cache_values, lengths, jnp.swapaxes(new_keys, 0, 1), jnp.swapaxes(new_values, 0, 1)))
    return jnp.swapaxes(stacked, 0, 1)

def reference(short_inputs, long_inputs, short_keys, short_values, long_keys, long_values, short_lengths, long_lengths, attn_gain, mlp_gain, query_scale, q_weight, k_weight, v_weight, o_weight, up_weight, down_weight):
    step_count, short_count, model_width = short_inputs.shape
    head_count, head_dim = query_scale.shape
    all_rows = jnp.concatenate([short_inputs, long_inputs], axis=1)
    flat_rows = all_rows.reshape(-1, model_width)
    normed = rms_scale(flat_rows.astype(jnp.float32), attn_gain).astype(jnp.bfloat16)
    queries = (project_heads(normed, q_weight, step_count, head_count) * query_scale * head_dim ** (-0.5)).astype(jnp.bfloat16)
    new_keys = project_heads(normed, k_weight, step_count, head_count).astype(jnp.bfloat16)
    new_values = project_heads(normed, v_weight, step_count, head_count).astype(jnp.bfloat16)
    short_out = attend_group(queries[:, :short_count], short_keys, short_values, short_lengths, new_keys[:, :short_count], new_values[:, :short_count])
    long_out = attend_group(queries[:, short_count:], long_keys, long_values, long_lengths, new_keys[:, short_count:], new_values[:, short_count:])
    attended = jnp.concatenate([short_out, long_out], axis=1).reshape(flat_rows.shape[0], -1)
    residual_mid = flat_rows.astype(jnp.float32) + jnp.dot(attended, o_weight, preferred_element_type=jnp.float32)
    normed_mid = rms_scale(residual_mid, mlp_gain).astype(jnp.bfloat16)
    hidden = jax.nn.silu(jnp.dot(normed_mid, up_weight, preferred_element_type=jnp.float32)).astype(jnp.bfloat16)
    output = residual_mid + jnp.dot(hidden, down_weight, preferred_element_type=jnp.float32)
    output = output.astype(jnp.bfloat16).reshape(step_count, -1, model_width)
    return (output[:, :short_count], output[:, short_count:])
```

```python
import functools

import jax
import jax.numpy as jnp
from jax import lax
from jax.experimental import pallas as pl
from jax.experimental.pallas import tpu as pltpu
from jax.sharding import PartitionSpec as P

norm_eps = 1e-06
masked_fill = -1e30
MESH = pl.DeviceIdType.MESH
F32 = jnp.float32
BF16 = jnp.bfloat16
TP = 4
RING = 4
STEPS = 4
HEADS = 4
HD = 80
WIDE = HEADS * HD
GROUP = 16
SLOTS = 16
ROWS = GROUP * STEPS


def rms_rows(rows, gain):
    mean_square = jnp.sum(rows * rows, axis=-1, keepdims=True) / rows.shape[-1]
    return rows * lax.rsqrt(mean_square + norm_eps) * gain


def dot_f32(a, b):
    return jnp.dot(a, b, preferred_element_type=F32)


def head_select(pieces, lane_head):
    out = pieces[0]
    for head in range(1, HEADS):
        out = jnp.where(lane_head == head, pieces[head], out)
    return out


def layer_kernel(
    chunk,
    n_long,
    x_hbm,
    xl_ref,
    sk_hbm,
    sv_hbm,
    lk_ref,
    lv_ref,
    slen_ref,
    llen_ref,
    again_ref,
    mgain_ref,
    qscale_ref,
    wq_hbm,
    wk_hbm,
    wv_hbm,
    wo_hbm,
    wu_hbm,
    wd_hbm,
    out_hbm,
    outl_ref,
    xv,
    kc,
    vc,
    wqkv,
    wod,
    wup,
    att_s,
    att_r,
    attl_s,
    attl_r,
    att_cat,
    xlp,
    qb,
    kb,
    vb,
    code,
    lens,
    part,
    part_r,
    out_s,
    outl_s,
    outl_r,
    loc_sem,
    zs_send,
    zs_recv,
    ring_send,
    ring_recv,
    cx_send,
    cx_recv,
    att_send,
    att_recv,
    attl_send,
    attl_recv,
    long_send,
    long_recv,
    out_send,
    out_recv,
    outl_send,
    outl_recv,
):
    z = lax.axis_index("tp")
    j = lax.axis_index("seq")
    core = j % 2
    chip = j // 2
    cx = chip % RING
    cy = chip // RING
    crows = STEPS * chunk

    def x_peer(k):
        return (cy * RING + (cx + k) % RING) * 2 + core

    def y_peer(k):
        return (((cy + k) % RING) * RING + cx) * 2 + core

    def ring_peer(k):
        return (1 - core) * x_peer(k) + core * y_peer(k)

    partner = chip * 2 + (1 - core)
    ring_pos = (1 - core) * cx + core * cy

    def z_peer(k):
        return (z + k) % TP

    order = (2, 1, 3, 0)

    sem_at = 0
    local = {}

    def start_local(name, src, dst):
        local[name] = pltpu.make_async_copy(src, dst, loc_sem.at[len(local)])
        local[name].start()

    start_local("wo", wo_hbm, wod.at[0, z])
    start_local("wd", wd_hbm, wod.at[1, z])
    start_local("wu", wu_hbm, wup.at[z])
    for i, w in enumerate((wq_hbm, wk_hbm, wv_hbm)):
        start_local("w%d" % i, w, wqkv.at[i])
    for i, k in enumerate(order):
        at = pl.ds(pl.multiple_of(z_peer(k) * chunk, 16), chunk)
        start_local("x%d" % i, x_hbm.at[:, at, :], xv.at[i])
        start_local("k%d" % i, sk_hbm.at[at], kc.at[i])
        start_local("v%d" % i, sv_hbm.at[at], vc.at[i])

    barrier = pltpu.get_barrier_semaphore()
    for k in range(1, 4):
        for dev in ((j, z_peer(k)), (x_peer(k), z), (y_peer(k), z)):
            pl.semaphore_signal(barrier, inc=1, device_id=dev, device_id_type=MESH)
    pl.semaphore_signal(barrier, inc=1, device_id=(partner, z), device_id_type=MESH)
    pl.semaphore_wait(barrier, 10)

    def remote(src, dst, send, recv, dev):
        return pltpu.make_async_remote_copy(
            src_ref=src, dst_ref=dst, send_sem=send, recv_sem=recv, device_id=dev, device_id_type=MESH
        )

    def od_piece(src_z):
        return wod.at[core, src_z, pl.ds(pl.multiple_of(ring_pos * 80, 16), 80)]

    def up_piece(src_z):
        return wup.at[src_z, pl.ds(pl.multiple_of(core * 640 + ring_pos * 160, 16), 160)]

    pieces = (od_piece, up_piece)

    local["wo"].wait()
    local["wd"].wait()
    local["wu"].wait()
    zs = [[], []]
    for arr in range(2):
        for k in (2, 1, 3):
            ref = pieces[arr](z)
            copy = remote(ref, ref, zs_send.at[arr, k - 1], zs_recv.at[arr, k - 1], (j, z_peer(k)))
            copy.start()
            zs[arr].append(copy)

    ring = [[], []]

    def start_ring(arr):
        for copy in zs[arr]:
            copy.wait()
        for k in (1, 3, 2):
            src_z = z_peer(k)
            for step in (1, 3, 2):
                ref = pieces[arr](src_z)
                copy = remote(
                    ref,
                    ref,
                    ring_send.at[arr, k - 1, step - 1],
                    ring_recv.at[arr, k - 1, step - 1],
                    (ring_peer(step), z),
                )
                copy.start()
                ring[arr].append(copy)

    crossed = [[], []]

    def start_cross(arr):
        for copy in ring[arr]:
            copy.wait()
        for k in (1, 3, 2):
            src_z = z_peer(k)
            if arr == 0:
                ref = wod.at[core, src_z]
            else:
                ref = wup.at[src_z, pl.ds(pl.multiple_of(core * 640, 16), 640)]
            copy = remote(ref, ref, cx_send.at[arr, k - 1], cx_recv.at[arr, k - 1], (partner, z))
            copy.start()
            crossed[arr].append(copy)

    lane_head = lax.broadcasted_iota(jnp.int32, (ROWS, WIDE), 1) // HD
    row_head = lax.broadcasted_iota(jnp.int32, (1, WIDE), 1) // HD
    head_keep = [(row_head == head).astype(F32).astype(BF16) for head in range(HEADS)]
    row_i = lax.broadcasted_iota(jnp.int32, (ROWS, GROUP * SLOTS), 0)
    col_i = lax.broadcasted_iota(jnp.int32, (ROWS, GROUP * SLOTS), 1)
    code_cached = jnp.where(col_i // SLOTS == row_i % GROUP, col_i % SLOTS, 1000)
    row_f = lax.broadcasted_iota(jnp.int32, (ROWS, ROWS), 0)
    col_f = lax.broadcasted_iota(jnp.int32, (ROWS, ROWS), 1)
    fresh_ok = (col_f % GROUP == row_f % GROUP) & (col_f // GROUP <= row_f // GROUP)
    code_fresh = jnp.where(fresh_ok, -1, 1000)
    code[:, 0 : GROUP * SLOTS] = code_cached
    code[:, GROUP * SLOTS :] = code_fresh

    def len_column(len_row, count, first):
        shape = (count, len_row.shape[1])
        eq = lax.broadcasted_iota(jnp.int32, shape, 1) == lax.broadcasted_iota(jnp.int32, shape, 0) + first
        picked = jnp.sum(jnp.where(eq, len_row, 0).astype(F32), axis=1, keepdims=True)
        return picked.astype(jnp.int32)

    n_short = slen_ref.shape[1]
    lens[...] = jnp.broadcast_to(len_column(slen_ref[...], n_short, 0), lens.shape)

    def project(rows, count):
        normed = rms_rows(rows, again_ref[...]).astype(BF16)
        q = dot_f32(normed, wqkv[0]) * qscale_ref[...] * HD ** (-0.5)
        qb[0:count, :] = q.astype(BF16)
        kb[0:count, :] = dot_f32(normed, wqkv[1]).astype(BF16)
        vb[0:count, :] = dot_f32(normed, wqkv[2]).astype(BF16)

    def attend(q_rows, keys, values, limit, long):
        wide_q = jnp.concatenate([q_rows * head_keep[head] for head in range(HEADS)], axis=0)
        scores = lax.dot_general(wide_q, keys, (((1,), (1,)), ((), ())), preferred_element_type=F32)
        codes = code[...]
        if long:
            lane = lax.broadcasted_iota(jnp.int32, (ROWS, WIDE), 1)
            fresh_off = (lane >= GROUP * SLOTS).astype(jnp.int32) * (jnp.minimum(j, 1) * 1000)
            codes = codes + fresh_off
        lim = jnp.concatenate([limit] * STEPS, axis=0)
        bias = jnp.where(codes < lim, 0.0, masked_fill)
        valid = jnp.concatenate([bias] * HEADS, axis=0) == 0.0
        scores = jnp.where(valid, scores, masked_fill)
        top = jnp.max(scores, axis=1, keepdims=True)
        probs = jnp.exp(scores - top)
        if long:
            probs = jnp.where(valid, probs, 0.0)
        total = jnp.sum(probs, axis=1, keepdims=True)
        weighted = dot_f32(probs.astype(BF16), values)
        cut = lambda a: [a[head * ROWS : (head + 1) * ROWS] for head in range(HEADS)]
        return cut(top), cut(total), head_select(cut(weighted), lane_head)

    for i in range(3):
        local["w%d" % i].wait()
    xlp[...] = jnp.zeros_like(xlp)
    for s in range(STEPS):
        xlp[s, 0:n_long, :] = xl_ref[s].astype(F32)
    project(xlp[...].reshape(ROWS, xlp.shape[-1]), ROWS)
    pad = jnp.zeros((GROUP * SLOTS - n_long * SLOTS, WIDE), BF16)
    long_keys = jnp.concatenate([lk_ref[...].reshape(n_long * SLOTS, WIDE), pad, kb[0:ROWS, :]], axis=0)
    long_values = jnp.concatenate([lv_ref[...].reshape(n_long * SLOTS, WIDE), pad, vb[0:ROWS, :]], axis=0)
    long_limit = jnp.clip(len_column(llen_ref[...], GROUP, 0) - j * SLOTS, 0, SLOTS)
    top, total, weighted = attend(qb[0:ROWS, :], long_keys, long_values, long_limit, True)
    stat_lane = lax.broadcasted_iota(jnp.int32, (ROWS, 128), 1)

    def pack_part(slot, top, total, weighted):
        stats = jnp.zeros((ROWS, 128), F32)
        for head in range(HEADS):
            stats = jnp.where(stat_lane == head, top[head], stats)
            stats = jnp.where(stat_lane == HEADS + head, total[head], stats)
        part[slot, :, 0:128] = stats
        part[slot, :, 128 : 128 + WIDE] = weighted

    def merge_parts(refs):
        stats = [r[:, 0:128] for r in refs]
        tops = [[s[:, head : head + 1] for s in stats] for head in range(HEADS)]
        totals = [[s[:, HEADS + head : HEADS + head + 1] for s in stats] for head in range(HEADS)]
        best, summed, scales = [], [], []
        for head in range(HEADS):
            m = functools.reduce(jnp.maximum, tops[head])
            sc = [jnp.exp(t - m) for t in tops[head]]
            best.append(m)
            scales.append(sc)
            summed.append(sum(t * f for t, f in zip(totals[head], sc)))
        weighted = 0.0
        for i, r in enumerate(refs):
            factor = head_select([jnp.broadcast_to(scales[h][i], (ROWS, WIDE)) for h in range(HEADS)], lane_head)
            weighted = weighted + r[:, 128 : 128 + WIDE] * factor
        return best, summed, weighted

    part[...] = jnp.zeros_like(part)
    pack_part(0, top, total, weighted)

    def long_copy(slot, index, dev):
        copy = remote(part.at[slot], part_r.at[index], long_send.at[index], long_recv.at[index], dev)
        copy.start()
        return copy

    long_copies = [[long_copy(0, 0, (partner, z))], [], []]

    def short_chunk(i, dst):
        local["x%d" % i].wait()
        local["k%d" % i].wait()
        local["v%d" % i].wait()
        project(xv[i].reshape(crows, xv.shape[-1]).astype(F32), crows)
        first = z_peer(order[i]) * chunk

        def body(g, carry):
            base = pl.multiple_of(g * GROUP, GROUP)
            rows = lambda ref: jnp.concatenate(
                [ref[pl.ds(pl.multiple_of(s * chunk + base, GROUP), GROUP), :] for s in range(STEPS)], axis=0
            )
            limit = lens[pl.ds(pl.multiple_of(first + base, GROUP), GROUP), 0:1]
            keys = jnp.concatenate([kc[i, pl.ds(base, GROUP)].reshape(GROUP * SLOTS, WIDE), rows(kb)], axis=0)
            values = jnp.concatenate([vc[i, pl.ds(base, GROUP)].reshape(GROUP * SLOTS, WIDE), rows(vb)], axis=0)
            top, total, weighted = attend(rows(qb), keys, values, limit, False)
            denom = head_select([jnp.broadcast_to(t, (ROWS, WIDE)) for t in total], lane_head)
            done = (weighted / denom).astype(BF16)
            for s in range(STEPS):
                dst[pl.ds(pl.multiple_of(s * chunk + base, GROUP), GROUP), :] = done[s * GROUP : (s + 1) * GROUP]
            return carry

        lax.fori_loop(0, chunk // GROUP, body, 0)

    att_copies = []

    def send_att(i):
        k = order[i]
        copy = remote(att_s.at[i], att_r.at[z], att_send.at[i], att_recv.at[i], (j, z_peer(k)))
        copy.start()
        att_copies.append(copy)

    short_chunk(0, att_s.at[0])
    send_att(0)
    start_ring(0)
    for copy in long_copies[0]:
        copy.wait()
    pack_part(1, *merge_parts([part.at[0], part_r.at[0]]))
    for k in range(1, 4):
        long_copies[1].append(long_copy(1, k, (x_peer(k), z)))

    short_chunk(1, att_s.at[1])
    send_att(1)
    start_ring(1)
    for copy in long_copies[1]:
        copy.wait()
    pack_part(2, *merge_parts([part.at[1]] + [part_r.at[k] for k in range(1, 4)]))
    for k in range(1, 4):
        long_copies[2].append(long_copy(2, 3 + k, (y_peer(k), z)))

    short_chunk(2, att_s.at[2])
    send_att(2)
    for copy in long_copies[2]:
        copy.wait()
    top, total, weighted = merge_parts([part.at[2]] + [part_r.at[3 + k] for k in range(1, 4)])
    denom = head_select([jnp.broadcast_to(t, (ROWS, WIDE)) for t in total], lane_head)
    done = (weighted / jnp.where(denom == 0.0, 1.0, denom)).astype(BF16)
    for s in range(STEPS):
        attl_s[s] = done[s * GROUP : (s + 1) * GROUP]
    attl_r[z] = attl_s[z]
    for i in range(3):
        to = z_peer(order[i])
        copy = remote(attl_s.at[to], attl_r.at[z], attl_send.at[i], attl_recv.at[i], (j, to))
        copy.start()
        att_copies.append(copy)

    short_chunk(3, att_r.at[z])
    start_cross(0)
    start_cross(1)

    for copy in att_copies:
        copy.wait()
    att_cat[0:crows, :] = jnp.concatenate([att_r[s] for s in range(TP)], axis=1)
    att_cat[crows:, :] = jnp.concatenate([attl_r[s] for s in range(TP)], axis=1)
    for copy in crossed[0]:
        copy.wait()
    model = xv.shape[-1]
    x_rows = jnp.concatenate([xv[3].reshape(crows, model).astype(F32), xlp[z]], axis=0)
    mid = x_rows + dot_f32(att_cat[...], wod[0].reshape(model, model))
    normed = rms_rows(mid, mgain_ref[...]).astype(BF16)
    for copy in crossed[1]:
        copy.wait()
    hidden = []
    for s in range(TP):
        pre = dot_f32(normed, wup[s])
        hidden.append((pre / (1.0 + jnp.exp(-pre))).astype(BF16))
    att_cat[...] = jnp.concatenate(hidden, axis=1)
    result = mid + dot_f32(att_cat[...], wod[1].reshape(model, model))
    for s in range(TP):
        share = result[:, s * WIDE : (s + 1) * WIDE].astype(BF16)
        out_s[s] = share[0:crows].reshape(STEPS, chunk, WIDE)
        outl_s[s] = share[crows:]

    here = pl.ds(pl.multiple_of(z * chunk, 16), chunk)
    last = []
    for i in range(3):
        to = z_peer(order[i])
        copy = remote(out_s.at[to], out_hbm.at[:, here, :], out_send.at[i], out_recv.at[i], (j, to))
        copy.start()
        last.append(copy)
        copy = remote(outl_s.at[to], outl_r.at[z], outl_send.at[i], outl_recv.at[i], (j, to))
        copy.start()
        last.append(copy)
    own = pltpu.make_async_copy(out_s.at[z], out_hbm.at[:, here, :], loc_sem.at[len(local)])
    own.start()
    outl_r[z] = outl_s[z]
    own.wait()
    for copy in last:
        copy.wait()
    outl_ref[...] = outl_r[:, 0:n_long, :]


def per_device(
    short_inputs,
    long_inputs,
    short_keys,
    short_values,
    long_keys,
    long_values,
    short_lengths,
    long_lengths,
    attn_gain,
    mlp_gain,
    query_scale,
    q_weight,
    k_weight,
    v_weight,
    o_weight,
    up_weight,
    down_weight,
):
    steps, n_short, model = short_inputs.shape
    n_long = long_inputs.shape[1]
    chunk = n_short // TP
    crows = steps * chunk
    any_spec = pl.BlockSpec(memory_space=pl.ANY)
    vm = pl.BlockSpec(memory_space=pltpu.VMEM)
    dma = pltpu.SemaphoreType.DMA
    V = pltpu.VMEM
    out_shape = (
        jax.ShapeDtypeStruct((steps, n_short, WIDE), BF16),
        jax.ShapeDtypeStruct((steps, n_long, WIDE), BF16),
    )
    return pl.pallas_call(
        functools.partial(layer_kernel, chunk, n_long),
        out_shape=out_shape,
        in_specs=[any_spec, vm, any_spec, any_spec, vm, vm, vm, vm, vm, vm, vm] + [any_spec] * 6,
        out_specs=(any_spec, vm),
        scratch_shapes=[
            V((4, steps, chunk, model), BF16),
            V((4, chunk, SLOTS, WIDE), BF16),
            V((4, chunk, SLOTS, WIDE), BF16),
            V((3, model, WIDE), BF16),
            V((2, TP, WIDE, model), BF16),
            V((TP, model, WIDE), BF16),
            V((3, crows, WIDE), BF16),
            V((TP, crows, WIDE), BF16),
            V((STEPS, GROUP, WIDE), BF16),
            V((TP, GROUP, WIDE), BF16),
            V((crows + GROUP, model), BF16),
            V((STEPS, GROUP, model), F32),
            V((crows, WIDE), BF16),
            V((crows, WIDE), BF16),
            V((crows, WIDE), BF16),
            V((ROWS, GROUP * SLOTS + ROWS), jnp.int32),
            V((n_short, 128), jnp.int32),
            V((3, ROWS, 512), F32),
            V((7, ROWS, 512), F32),
            V((TP, steps, chunk, WIDE), BF16),
            V((TP, GROUP, WIDE), BF16),
            V((TP, GROUP, WIDE), BF16),
            dma((19,)),
            dma((2, 3)),
            dma((2, 3)),
            dma((2, 3, 3)),
            dma((2, 3, 3)),
            dma((2, 3)),
            dma((2, 3)),
            dma((3,)),
            dma((3,)),
            dma((3,)),
            dma((3,)),
            dma((7,)),
            dma((7,)),
            dma((3,)),
            dma((3,)),
            dma((3,)),
            dma((3,)),
        ],
        compiler_params=pltpu.CompilerParams(
            collective_id=0, has_side_effects=True, vmem_limit_bytes=60 * 2**20
        ),
        name="layer",
    )(
        short_inputs,
        long_inputs,
        short_keys,
        short_values,
        long_keys,
        long_values,
        short_lengths.reshape(1, n_short),
        long_lengths.reshape(1, n_long),
        attn_gain.reshape(1, model),
        mlp_gain.reshape(1, model),
        query_scale.reshape(1, WIDE),
        q_weight,
        k_weight,
        v_weight,
        o_weight,
        up_weight,
        down_weight,
    )


def solution(mesh):
    return jax.shard_map(
        per_device,
        mesh=mesh,
        in_specs=(
            P(None, "seq", None),
            P(),
            P("seq", None, "tp"),
            P("seq", None, "tp"),
            P(None, "seq", "tp"),
            P(None, "seq", "tp"),
            P("seq"),
            P(),
            P(),
            P(),
            P("tp", None),
            P(None, "tp"),
            P(None, "tp"),
            P(None, "tp"),
            P("tp", None),
            P(None, "tp"),
            P("tp", None),
        ),
        out_specs=(P(None, "seq", "tp"), P(None, None, "tp")),
        check_vma=False,
    )
```

```python
import functools

import jax
import jax.numpy as jnp
from jax import lax
from jax.experimental import pallas as pl
from jax.experimental.pallas import tpu as pltpu
from jax.sharding import PartitionSpec as P

norm_eps = 1e-06
masked_fill = -1e30
MESH = pl.DeviceIdType.MESH
F32 = jnp.float32
BF16 = jnp.bfloat16
TP = 4
RING = 4
STEPS = 4
HEADS = 4
HD = 80
WIDE = HEADS * HD
PITCH = 384
GROUP = 16
SLOTS = 16
ROWS = GROUP * STEPS


def rms_rows(rows, gain):
    mean_square = jnp.sum(rows * rows, axis=-1, keepdims=True) / rows.shape[-1]
    return rows * lax.rsqrt(mean_square + norm_eps) * gain


def dot_f32(a, b):
    return jnp.dot(a, b, preferred_element_type=F32)


def dot_t(a, b):
    return lax.dot_general(a, b, (((1,), (1,)), ((), ())), preferred_element_type=F32)


def head_select(pieces, lane_head):
    out = pieces[0]
    for head in range(1, HEADS):
        out = jnp.where(lane_head == head, pieces[head], out)
    return out


def layer_kernel(
    chunk,
    n_long,
    x_hbm,
    xl_ref,
    sk_hbm,
    sv_hbm,
    lk_ref,
    lv_ref,
    slen_ref,
    llen_ref,
    again_ref,
    mgain_ref,
    qscale_ref,
    wq_hbm,
    wk_hbm,
    wv_hbm,
    wo_hbm,
    wu_hbm,
    wd_hbm,
    out_hbm,
    outl_ref,
    xv,
    kc,
    vc,
    wqkv,
    w3,
    att_s,
    att_r,
    attl_s,
    attl_r,
    att_cat,
    xlp,
    qb,
    kb,
    vb,
    code,
    lens,
    part,
    part_r,
    out_s,
    outl_s,
    outl_r,
    loc_sem,
    zs_send,
    zs_recv,
    ring_send,
    ring_recv,
    cx_send,
    cx_recv,
    att_send,
    att_recv,
    attl_send,
    attl_recv,
    long_send,
    long_recv,
    out_send,
    out_recv,
    outl_send,
    outl_recv,
):
    z = lax.axis_index("tp")
    j = lax.axis_index("seq")
    core = j % 2
    chip = j // 2
    cx = chip % RING
    cy = chip // RING
    crows = STEPS * chunk

    def x_peer(k):
        return (cy * RING + (cx + k) % RING) * 2 + core

    def y_peer(k):
        return (((cy + k) % RING) * RING + cx) * 2 + core

    def ring_peer(k):
        return (1 - core) * x_peer(k) + core * y_peer(k)

    partner = chip * 2 + (1 - core)
    ring_pos = (1 - core) * cx + core * cy

    def z_peer(k):
        return (z + k) % TP

    order = (2, 1, 3, 0)

    sem_at = 0
    local = {}

    def start_local(name, src, dst):
        local[name] = pltpu.make_async_copy(src, dst, loc_sem.at[len(local)])
        local[name].start()

    for i, w in enumerate((wo_hbm, wu_hbm, wd_hbm)):
        start_local("g%d" % i, w, w3.at[i, z])
    for i, w in enumerate((wq_hbm, wk_hbm, wv_hbm)):
        start_local("w%d" % i, w, wqkv.at[pl.ds(PITCH * i, WIDE)])
    for i, k in enumerate(order):
        at = pl.ds(pl.multiple_of(z_peer(k) * chunk, 16), chunk)
        start_local("x%d" % i, x_hbm.at[:, at, :], xv.at[i])
        start_local("k%d" % i, sk_hbm.at[at], kc.at[i])
        start_local("v%d" % i, sv_hbm.at[at], vc.at[i])

    barrier = pltpu.get_barrier_semaphore()
    for k in range(1, 4):
        for dev in ((j, z_peer(k)), (x_peer(k), z), (y_peer(k), z)):
            pl.semaphore_signal(barrier, inc=1, device_id=dev, device_id_type=MESH)
    pl.semaphore_signal(barrier, inc=1, device_id=(partner, z), device_id_type=MESH)
    pl.semaphore_wait(barrier, 10)

    def remote(src, dst, send, recv, dev):
        return pltpu.make_async_remote_copy(
            src_ref=src, dst_ref=dst, send_sem=send, recv_sem=recv, device_id=dev, device_id_type=MESH
        )

    half = WIDE // 2
    quarter = half // RING

    def piece(arr, src_z):
        return w3.at[arr, src_z, pl.ds(pl.multiple_of(core * half + ring_pos * quarter, 8), quarter)]

    zs = [[], [], []]
    for arr in range(3):
        local["g%d" % arr].wait()
        for k in (2, 1, 3):
            ref = piece(arr, z)
            copy = remote(ref, ref, zs_send.at[arr, k - 1], zs_recv.at[arr, k - 1], (j, z_peer(k)))
            copy.start()
            zs[arr].append(copy)

    ring = [[], [], []]

    def start_ring(arr):
        for copy in zs[arr]:
            copy.wait_recv()
        for k in (1, 3, 2):
            src_z = z_peer(k)
            for step in (1, 3, 2):
                ref = piece(arr, src_z)
                copy = remote(
                    ref,
                    ref,
                    ring_send.at[arr, k - 1, step - 1],
                    ring_recv.at[arr, k - 1, step - 1],
                    (ring_peer(step), z),
                )
                copy.start()
                ring[arr].append(copy)

    crossed = [[], [], []]

    def start_cross(arr):
        for copy in ring[arr]:
            copy.wait_recv()
        for k in (1, 3, 2):
            src_z = z_peer(k)
            ref = w3.at[arr, src_z, pl.ds(pl.multiple_of(core * half, 16), half)]
            copy = remote(ref, ref, cx_send.at[arr, k - 1], cx_recv.at[arr, k - 1], (partner, z))
            copy.start()
            crossed[arr].append(copy)

    q_scale = jnp.concatenate([qscale_ref[head : head + 1, :] for head in range(HEADS)], axis=1)
    lane_head = lax.broadcasted_iota(jnp.int32, (ROWS, WIDE), 1) // HD
    row_head = lax.broadcasted_iota(jnp.int32, (1, WIDE), 1) // HD
    head_keep = [(row_head == head).astype(F32).astype(BF16) for head in range(HEADS)]
    row_i = lax.broadcasted_iota(jnp.int32, (ROWS, GROUP * SLOTS), 0)
    col_i = lax.broadcasted_iota(jnp.int32, (ROWS, GROUP * SLOTS), 1)
    code_cached = jnp.where(col_i // SLOTS == row_i % GROUP, col_i % SLOTS, 1000)
    row_f = lax.broadcasted_iota(jnp.int32, (ROWS, ROWS), 0)
    col_f = lax.broadcasted_iota(jnp.int32, (ROWS, ROWS), 1)
    fresh_ok = (col_f % GROUP == row_f % GROUP) & (col_f // GROUP <= row_f // GROUP)
    code_fresh = jnp.where(fresh_ok, -1, 1000)
    code[:, 0 : GROUP * SLOTS] = code_cached
    code[:, GROUP * SLOTS :] = code_fresh

    def len_column(len_row, count, first):
        shape = (count, len_row.shape[1])
        eq = lax.broadcasted_iota(jnp.int32, shape, 1) == lax.broadcasted_iota(jnp.int32, shape, 0) + first
        picked = jnp.sum(jnp.where(eq, len_row, 0).astype(F32), axis=1, keepdims=True)
        return picked.astype(jnp.int32)

    n_short = slen_ref.shape[0]
    lens[...] = jnp.broadcast_to(len_column(slen_ref[...].reshape(1, n_short), n_short, 0), lens.shape)

    def project(rows, count):
        normed = rms_rows(rows, again_ref[...].reshape(1, -1)).astype(BF16)
        qkv = dot_t(normed, wqkv[...])
        q = qkv[:, 0:WIDE] * q_scale * HD ** (-0.5)
        qb[0:count, :] = q.astype(BF16)
        kb[0:count, :] = qkv[:, PITCH : PITCH + WIDE].astype(BF16)
        vb[0:count, :] = qkv[:, 2 * PITCH : 2 * PITCH + WIDE].astype(BF16)

    def attend(q_rows, keys, values, limit, long):
        wide_q = jnp.concatenate([q_rows * head_keep[head] for head in range(HEADS)], axis=0)
        scores = dot_t(wide_q, keys)
        codes = code[...]
        if long:
            lane = lax.broadcasted_iota(jnp.int32, (ROWS, WIDE), 1)
            fresh_off = (lane >= GROUP * SLOTS).astype(jnp.int32) * (jnp.minimum(j, 1) * 1000)
            codes = codes + fresh_off
        lim = jnp.concatenate([limit] * STEPS, axis=0)
        bias = jnp.where(codes < lim, 0.0, masked_fill)
        valid = jnp.concatenate([bias] * HEADS, axis=0) == 0.0
        scores = jnp.where(valid, scores, masked_fill)
        top = jnp.max(scores, axis=1, keepdims=True)
        probs = jnp.exp(scores - top)
        if long:
            probs = jnp.where(valid, probs, 0.0)
        total = jnp.sum(probs, axis=1, keepdims=True)
        weighted = dot_f32(probs.astype(BF16), values)
        cut = lambda a: [a[head * ROWS : (head + 1) * ROWS] for head in range(HEADS)]
        return cut(top), cut(total), head_select(cut(weighted), lane_head)

    for i in range(3):
        local["w%d" % i].wait()
    xlp[...] = jnp.zeros_like(xlp)
    for b in range(n_long):
        request = xl_ref[b].astype(F32)
        for s in range(STEPS):
            xlp[s, b : b + 1, :] = request[s : s + 1]
    project(xlp[...].reshape(ROWS, xlp.shape[-1]), ROWS)
    pad = jnp.zeros((GROUP * SLOTS - n_long * SLOTS, WIDE), BF16)
    long_keys = jnp.concatenate([lk_ref[...].reshape(n_long * SLOTS, WIDE), pad, kb[0:ROWS, :]], axis=0)
    long_values = jnp.concatenate([lv_ref[...].reshape(n_long * SLOTS, WIDE), pad, vb[0:ROWS, :]], axis=0)
    long_limit = jnp.clip(len_column(llen_ref[...], GROUP, 0) - j * SLOTS, 0, SLOTS)
    top, total, weighted = attend(qb[0:ROWS, :], long_keys, long_values, long_limit, True)
    stat_lane = lax.broadcasted_iota(jnp.int32, (ROWS, 128), 1)

    def pack_part(slot, top, total, weighted):
        stats = jnp.zeros((ROWS, 128), F32)
        for head in range(HEADS):
            stats = jnp.where(stat_lane == head, top[head], stats)
            stats = jnp.where(stat_lane == HEADS + head, total[head], stats)
        part[slot, :, 0:128] = stats
        part[slot, :, 128 : 128 + WIDE] = weighted

    def merge_parts(refs):
        stats = [r[:, 0:128] for r in refs]
        tops = [[s[:, head : head + 1] for s in stats] for head in range(HEADS)]
        totals = [[s[:, HEADS + head : HEADS + head + 1] for s in stats] for head in range(HEADS)]
        best, summed, scales = [], [], []
        for head in range(HEADS):
            m = functools.reduce(jnp.maximum, tops[head])
            sc = [jnp.exp(t - m) for t in tops[head]]
            best.append(m)
            scales.append(sc)
            summed.append(sum(t * f for t, f in zip(totals[head], sc)))
        weighted = 0.0
        for i, r in enumerate(refs):
            factor = head_select([jnp.broadcast_to(scales[h][i], (ROWS, WIDE)) for h in range(HEADS)], lane_head)
            weighted = weighted + r[:, 128 : 128 + WIDE] * factor
        return best, summed, weighted

    part[...] = jnp.zeros_like(part)
    pack_part(0, top, total, weighted)

    def long_copy(slot, index, dev):
        copy = remote(part.at[slot], part_r.at[index], long_send.at[index], long_recv.at[index], dev)
        copy.start()
        return copy

    long_copies = [[long_copy(0, 0, (partner, z))], [], []]

    def short_chunk(i, dst, hooks=(None, None)):
        local["x%d" % i].wait()
        local["k%d" % i].wait()
        local["v%d" % i].wait()
        project(xv[i].reshape(crows, xv.shape[-1]).astype(F32), crows)
        first = z_peer(order[i]) * chunk
        if hooks[0] is not None:
            hooks[0]()

        def body(g, carry):
            base = pl.multiple_of(g * GROUP, GROUP)
            rows = lambda ref: jnp.concatenate(
                [ref[pl.ds(pl.multiple_of(s * chunk + base, GROUP), GROUP), :] for s in range(STEPS)], axis=0
            )
            limit = lens[pl.ds(pl.multiple_of(first + base, GROUP), GROUP), 0:1]
            keys = jnp.concatenate([kc[i, pl.ds(base, GROUP)].reshape(GROUP * SLOTS, WIDE), rows(kb)], axis=0)
            values = jnp.concatenate([vc[i, pl.ds(base, GROUP)].reshape(GROUP * SLOTS, WIDE), rows(vb)], axis=0)
            top, total, weighted = attend(rows(qb), keys, values, limit, False)
            denom = head_select([jnp.broadcast_to(t, (ROWS, WIDE)) for t in total], lane_head)
            done = (weighted / denom).astype(BF16)
            for s in range(STEPS):
                dst[pl.ds(pl.multiple_of(s * chunk + base, GROUP), GROUP), :] = done[s * GROUP : (s + 1) * GROUP]
            return carry

        groups = chunk // GROUP
        lax.fori_loop(0, groups // 2, body, 0)
        if hooks[1] is not None:
            hooks[1]()
        lax.fori_loop(groups // 2, groups, body, 0)

    att_copies = []

    def send_att(i):
        k = order[i]
        copy = remote(att_s.at[i], att_r.at[z], att_send.at[i], att_recv.at[i], (j, z_peer(k)))
        copy.start()
        att_copies.append(copy)

    def long_to_x():
        long_copies[0][0].wait_recv()
        pack_part(1, *merge_parts([part.at[0], part_r.at[0]]))
        for k in range(1, 4):
            long_copies[1].append(long_copy(1, k, (x_peer(k), z)))

    def long_to_y():
        for copy in long_copies[1]:
            copy.wait_recv()
        pack_part(2, *merge_parts([part.at[1]] + [part_r.at[k] for k in range(1, 4)]))
        for k in range(1, 4):
            long_copies[2].append(long_copy(2, 3 + k, (y_peer(k), z)))

    def long_done():
        for copy in long_copies[2]:
            copy.wait_recv()
        top, total, weighted = merge_parts([part.at[2]] + [part_r.at[3 + k] for k in range(1, 4)])
        denom = head_select([jnp.broadcast_to(t, (ROWS, WIDE)) for t in total], lane_head)
        done = (weighted / jnp.where(denom == 0.0, 1.0, denom)).astype(BF16)
        for s in range(STEPS):
            attl_s[s] = done[s * GROUP : (s + 1) * GROUP]
        attl_r[z] = attl_s[z]
        for i in range(3):
            to = z_peer(order[i])
            copy = remote(attl_s.at[to], attl_r.at[z], attl_send.at[i], attl_recv.at[i], (j, to))
            copy.start()
            att_copies.append(copy)

    short_chunk(0, att_s.at[0], (long_to_x, lambda: start_ring(0)))
    send_att(0)
    short_chunk(1, att_s.at[1], (long_to_y, lambda: start_ring(1)))
    send_att(1)
    start_ring(2)
    short_chunk(2, att_s.at[2], (lambda: start_cross(0), long_done))
    send_att(2)
    short_chunk(3, att_r.at[z], (lambda: start_cross(1), None))
    start_cross(2)

    for copy in att_copies:
        copy.wait_recv()
    att_cat[0:crows, :] = jnp.concatenate([att_r[s] for s in range(TP)], axis=1)
    att_cat[crows:, :] = jnp.concatenate([attl_r[s] for s in range(TP)], axis=1)
    for copy in crossed[0]:
        copy.wait_recv()
    model = xv.shape[-1]
    x_rows = jnp.concatenate([xv[3].reshape(crows, model).astype(F32), xlp[z]], axis=0)
    mid = x_rows + dot_f32(att_cat[...], w3[0].reshape(model, model))
    normed = rms_rows(mid, mgain_ref[...].reshape(1, -1)).astype(BF16)
    for copy in crossed[1]:
        copy.wait_recv()
    pre = dot_t(normed, w3[1].reshape(model, model))
    att_cat[...] = (pre / (1.0 + jnp.exp(-pre))).astype(BF16)
    for copy in crossed[2]:
        copy.wait_recv()
    result = mid + dot_f32(att_cat[...], w3[2].reshape(model, model))
    for s in range(TP):
        share = result[:, s * WIDE : (s + 1) * WIDE].astype(BF16)
        out_s[s] = share[0:crows].reshape(STEPS, chunk, WIDE)
        outl_s[s] = share[crows:]

    here = pl.ds(pl.multiple_of(z * chunk, 16), chunk)
    last = []
    for i in range(3):
        to = z_peer(order[i])
        copy = remote(out_s.at[to], out_hbm.at[:, here, :], out_send.at[i], out_recv.at[i], (j, to))
        copy.start()
        last.append(copy)
        copy = remote(outl_s.at[to], outl_r.at[z], outl_send.at[i], outl_recv.at[i], (j, to))
        copy.start()
        last.append(copy)
    own = pltpu.make_async_copy(out_s.at[z], out_hbm.at[:, here, :], loc_sem.at[len(local)])
    own.start()
    outl_r[z] = outl_s[z]
    own.wait()
    for copy in last:
        copy.wait()
    for copies in zs + ring + crossed + long_copies + [att_copies]:
        for copy in copies:
            copy.wait_send()
    long_rows = [outl_r[s].astype(F32) for s in range(STEPS)]
    for b in range(n_long):
        rows = jnp.concatenate([long_rows[s][b : b + 1] for s in range(STEPS)], axis=0)
        outl_ref[b] = rows.astype(BF16)


def per_device(
    short_inputs,
    long_inputs,
    short_keys,
    short_values,
    long_keys,
    long_values,
    short_lengths,
    long_lengths,
    attn_gain,
    mlp_gain,
    query_scale,
    q_weight,
    k_weight,
    v_weight,
    o_weight,
    up_weight,
    down_weight,
):
    steps, n_short, model = short_inputs.shape
    n_long = long_inputs.shape[1]
    chunk = n_short // TP
    crows = steps * chunk
    any_spec = pl.BlockSpec(memory_space=pl.ANY)
    vm = pl.BlockSpec(memory_space=pltpu.VMEM)
    dma = pltpu.SemaphoreType.DMA
    V = pltpu.VMEM
    out_shape = (
        jax.ShapeDtypeStruct((steps, n_short, WIDE), BF16),
        jax.ShapeDtypeStruct((n_long, steps, WIDE), BF16),
    )
    short, long = pl.pallas_call(
        functools.partial(layer_kernel, chunk, n_long),
        out_shape=out_shape,
        in_specs=[any_spec, vm, any_spec, any_spec, vm, vm, vm, vm, vm, vm, vm] + [any_spec] * 6,
        out_specs=(any_spec, vm),
        scratch_shapes=[
            V((4, steps, chunk, model), BF16),
            V((4, chunk, SLOTS, WIDE), BF16),
            V((4, chunk, SLOTS, WIDE), BF16),
            V((2 * PITCH + WIDE, model), BF16),
            V((3, TP, WIDE, model), BF16),
            V((3, crows, WIDE), BF16),
            V((TP, crows, WIDE), BF16),
            V((STEPS, GROUP, WIDE), BF16),
            V((TP, GROUP, WIDE), BF16),
            V((crows + GROUP, model), BF16),
            V((STEPS, GROUP, model), F32),
            V((crows, WIDE), BF16),
            V((crows, WIDE), BF16),
            V((crows, WIDE), BF16),
            V((ROWS, GROUP * SLOTS + ROWS), jnp.int32),
            V((n_short, 128), jnp.int32),
            V((3, ROWS, 512), F32),
            V((7, ROWS, 512), F32),
            V((TP, steps, chunk, WIDE), BF16),
            V((TP, GROUP, WIDE), BF16),
            V((TP, GROUP, WIDE), BF16),
            dma((19,)),
            dma((3, 3)),
            dma((3, 3)),
            dma((3, 3, 3)),
            dma((3, 3, 3)),
            dma((3, 3)),
            dma((3, 3)),
            dma((3,)),
            dma((3,)),
            dma((3,)),
            dma((3,)),
            dma((7,)),
            dma((7,)),
            dma((3,)),
            dma((3,)),
            dma((3,)),
            dma((3,)),
        ],
        compiler_params=pltpu.CompilerParams(
            collective_id=0, has_side_effects=True, vmem_limit_bytes=60 * 2**20
        ),
        name="layer",
    )(
        short_inputs,
        jnp.swapaxes(long_inputs, 0, 1),
        short_keys,
        short_values,
        long_keys,
        long_values,
        short_lengths,
        long_lengths.reshape(1, n_long),
        attn_gain,
        mlp_gain,
        query_scale,
        q_weight.T,
        k_weight.T,
        v_weight.T,
        o_weight,
        up_weight.T,
        down_weight,
    )
    return short, jnp.swapaxes(long, 0, 1)


def solution(mesh):
    return jax.shard_map(
        per_device,
        mesh=mesh,
        in_specs=(
            P(None, "seq", None),
            P(),
            P("seq", None, "tp"),
            P("seq", None, "tp"),
            P(None, "seq", "tp"),
            P(None, "seq", "tp"),
            P("seq"),
            P(),
            P(),
            P(),
            P("tp", None),
            P(None, "tp"),
            P(None, "tp"),
            P(None, "tp"),
            P("tp", None),
            P(None, "tp"),
            P("tp", None),
        ),
        out_specs=(P(None, "seq", "tp"), P(None, None, "tp")),
        check_vma=False,
    )
```
